32 devices in a mesh: row: 4 (over y, x), col: 2 (over core), depth: 4 (over z).
Axes of the slice: x: 2, y: 2, z: 4, core: 2. Of those that a mesh axis runs over, the one named last changes fastest.
Arguments:
- source_desc: bfloat16 [2048, 256], P(('row', 'col', 'depth')), may hold values from -4 to 4
- target_desc: bfloat16 [16384, 256], P(('col', 'depth', 'row')), may hold values from -4 to 4
- target_dual: float32 [16384], P(('col', 'depth')), may hold values from -2 to 4.25
- row_weight: float32 [2048], P('row'), may hold values from 0.3 to 3
- matches: int32 [2048], P('row'), may hold values from 0 to 16383
Outputs:
- grad_source: float32 [2048, 256], P(('row', 'col', 'depth'))
- grad_target: float32 [16384, 256], P(('col', 'depth', 'row'))
The draws below stay inside these ranges and needn't reach their ends.
All inputs are finite; a program needn't handle non-finite values.
Results may differ from the reference program's by a relative error of at most 0.0029.
Values may be sent and summed in bfloat16 or wider, within the bound.
A program may use at most 64 MiB of HBM per device.

```python
import math
import jax
import jax.numpy as jnp
from jax import lax

D = 256
NS = 2048
NT = 16384


def base_desc(key, row_total):
    values = jax.random.normal(jax.random.fold_in(key, 2), (row_total, D), jnp.float32)
    return jnp.clip(values, -4.0, 4.0)


def draw_source_desc(key, part):
    values = base_desc(jax.random.fold_in(key, 11), NS)
    return values.astype(jnp.bfloat16)


def draw_target_desc(key, part):
    values = base_desc(jax.random.fold_in(key, 12), NT)
    return values.astype(jnp.bfloat16)


def draw_target_dual(key, part):
    position = jnp.arange(NT, dtype=jnp.float32) / NT
    jitter = jax.random.uniform(jax.random.fold_in(key, 21), (NT,), minval=-2.0, maxval=2.0)
    return jitter + 1.0986123 * position


def set_ends(drawn, own_key, low, largest):
    dims = drawn.shape
    place = [jax.random.randint(jax.random.fold_in(own_key, axis), (), 0, dims[axis]) for axis in range(len(dims))]
    drawn = drawn.at[tuple(place)].set(low)
    longest = dims.index(max(dims))
    place[longest] = (place[longest] + 1) % dims[longest]
    return drawn.at[tuple(place)].set(largest)


def levels(rng, extent, shards, low, largest):
    gain = 1.0
    for dim, parts in shards:
        heights = jax.random.uniform(jax.random.fold_in(jax.random.fold_in(rng, 6), dim), (parts,), jnp.float32, low / len(shards), largest / len(shards))
        gain = gain * jnp.repeat(jnp.exp(heights), extent[dim] // parts).reshape((-1,) + (1,) * (len(extent) - 1 - dim))
    return gain


def setup_inputs(seed: int = 0) -> dict:
    seeds = jax.random.split(jax.random.key(seed), 6)
    source_desc = draw_source_desc(jax.random.fold_in(seeds[5], 71), 0)
    target_desc = draw_target_desc(jax.random.fold_in(seeds[5], 71), 0)
    target_dual = draw_target_dual(jax.random.fold_in(seeds[5], 71), 0)
    row_weight = jnp.clip(jnp.exp(math.log(3.0) - 2.3025851 * jax.random.uniform(seeds[3], (NS,), jnp.float32) ** levels(seeds[3], (NS,), ((0, 4),), -0.2, 0.2)), 0.3, 3.0)
    matches = set_ends(jax.random.randint(seeds[4], (NS,), 0, NT), jax.random.fold_in(seeds[4], 1), 0, NT - 1).astype(jnp.int32)
    return {"source_desc": source_desc, "target_desc": target_desc, "target_dual": target_dual, "row_weight": row_weight, "matches": matches}


score_scale = 0.1875


def reference(source_desc, target_desc, target_dual, row_weight, matches):
    block_rows = math.gcd(NS, 512)
    columns = jnp.arange(NT, dtype=jnp.int32)

    def advance(tgt_grad, block_idx):
        start = (block_idx * block_rows).astype(jnp.int32)
        src_rows = lax.dynamic_slice_in_dim(source_desc, start, block_rows, 0)
        row_wts = lax.dynamic_slice_in_dim(row_weight, start, block_rows, 0)
        row_match = lax.dynamic_slice_in_dim(matches, start, block_rows, 0)
        scores = score_scale * jnp.dot(src_rows, target_desc.T, preferred_element_type=jnp.float32) + target_dual[None, :]
        highest = jnp.max(scores, axis=1, keepdims=True)
        log_total = highest + jnp.log(jnp.sum(jnp.exp(scores - highest), axis=1, keepdims=True))
        plan_tile = jnp.exp(scores - log_total)
        hit_mask = (columns[None, :] == row_match[:, None]).astype(jnp.float32)
        delta_tile = (row_wts[:, None] * (plan_tile - hit_mask)).astype(jnp.bfloat16)
        src_grad = score_scale * jnp.dot(delta_tile, target_desc, preferred_element_type=jnp.float32)
        tgt_grad = tgt_grad + score_scale * jnp.dot(delta_tile.T, src_rows, preferred_element_type=jnp.float32)
        return tgt_grad, src_grad

    tgt_grad, src_grad = lax.scan(advance, jnp.zeros((NT, D), jnp.float32), jnp.arange(NS // block_rows, dtype=jnp.int32))
    return src_grad.reshape(NS, D), tgt_grad
```

```python
import functools
import jax
import jax.numpy as jnp
from jax import lax
from jax.experimental import pallas as pl
from jax.experimental.pallas import tpu as pltpu
from jax.sharding import PartitionSpec as P

score_scale = 0.1875
F32 = jnp.float32
BF16 = jnp.bfloat16


def kernel(R, NC, ND, src, tgt, dual, wm, gs_out, gt_out,
           S, T2, dual2, wm_all, dcol, e_buf, m_buf, lamz, lamx, lamz_c, dbuf, ps, px, zs, zr,
           own_part, gt_send, gt_recv,
           s_pair, r_pair, s_z, r_z, s_x, r_x, s_wm, r_wm, s_lz, r_lz, s_lx, r_lx, s_p, r_p, s_zp, r_zp):
    G = (NC // 2) * ND
    n, D = src.shape
    own = tgt.shape[0]
    C = G * n
    row = lax.axis_index("row")
    col = lax.axis_index("col")
    dep = lax.axis_index("depth")
    par = lax.rem(col, 2)
    grp = (col // 2) * ND + dep
    sib_col = col + 1 - 2 * par

    def dev(r, c, d):
        return {"row": r, "col": c, "depth": d}

    sib = dev(row, sib_col, dep)

    def xpeer(k):
        r = lax.rem(row + k, R)
        return r, dev(r, col, dep)

    def zpeer(k):
        g = lax.rem(grp + k, G)
        return g, dev(row, (g // ND) * 2 + par, lax.rem(g, ND))

    def rcopy(a, b, ss, rs, to):
        return pltpu.make_async_remote_copy(src_ref=a, dst_ref=b, send_sem=ss, recv_sem=rs,
                                            device_id=to, device_id_type=pl.DeviceIdType.MESH)

    barrier = pltpu.get_barrier_semaphore()
    peers = [sib] + [xpeer(k)[1] for k in range(1, R)] + [zpeer(k)[1] for k in range(1, G)]
    for p in peers:
        pl.semaphore_signal(barrier, inc=1, device_id=p, device_id_type=pl.DeviceIdType.MESH)

    S[row, grp] = src[...]
    wm_all[row] = wm[...]
    dcol[0:own, :] = jnp.transpose(jnp.broadcast_to(dual[...], (128, own)))
    pl.semaphore_wait(barrier, len(peers))

    sends = []

    def go(c):
        c.start()
        sends.append(c)

    for k in range(1, G):
        g, to = zpeer(k)
        go(rcopy(src, S.at[row, grp], s_z.at[k], r_z.at[grp], to))
    for k in range(1, R):
        r, to = xpeer(k)
        go(rcopy(src, S.at[row, grp], s_x.at[k, 0], r_x.at[row, grp], to))
    go(rcopy(tgt, T2, s_pair.at[0], r_pair.at[0], sib))
    go(rcopy(dual, dual2, s_pair.at[1], r_pair.at[1], sib))
    for k in range(1, R):
        r, to = xpeer(k)
        go(rcopy(wm, wm_all.at[row], s_wm.at[k], r_wm.at[row], to))

    for k in range(1, G):
        g, to = zpeer(k)
        rcopy(src, S.at[row, g], s_z.at[k], r_z.at[g], to).wait_recv()
        for j in range(1, R):
            r, xto = xpeer(j)
            go(rcopy(S.at[row, g], S.at[row, g], s_x.at[j, k], r_x.at[row, g], xto))

    rcopy(dual, dual2, s_pair.at[1], r_pair.at[1], sib).wait_recv()
    dcol[own:2 * own, :] = jnp.transpose(jnp.broadcast_to(dual2[...], (128, own)))
    rcopy(tgt, T2, s_pair.at[0], r_pair.at[0], sib).wait_recv()

    lane_rep = C // 128

    def scores_chunk(r):
        rows = S[r].reshape(C, D)
        tops = []
        for h, t in ((0, tgt), (1, T2)):
            p = lax.dot_general(t[...], rows, (((1,), (1,)), ((), ())), preferred_element_type=F32)
            dc = dcol[h * own:(h + 1) * own, :]
            s = score_scale * p + jnp.concatenate([dc] * lane_rep, axis=1)
            e_buf[r, h * own:(h + 1) * own, :] = s
            tops.append(jnp.max(s, axis=0, keepdims=True))
        top = jnp.maximum(tops[0], tops[1])
        m_buf[r] = top
        e = jnp.exp(e_buf[r] - top)
        e_buf[r] = e
        lamz[grp, r] = top + jnp.log(jnp.sum(e, axis=0, keepdims=True))

    scores_chunk(row)

    def chunk_step(k, carry):
        r, to = xpeer(k)
        for g in range(G):
            rcopy(src, S.at[r, g], s_x.at[0, 0], r_x.at[r, g], to).wait_recv()
        scores_chunk(r)
        return carry

    lax.fori_loop(1, R, chunk_step, 0)

    def lse(parts):
        top = functools.reduce(jnp.maximum, parts)
        return top + jnp.log(functools.reduce(jnp.add, [jnp.exp(p - top) for p in parts]))

    for k in range(1, G):
        g, to = zpeer(k)
        go(rcopy(lamz.at[grp], lamz.at[grp], s_lz.at[k], r_lz.at[grp], to))
    for k in range(1, G):
        g, to = zpeer(k)
        rcopy(lamz.at[g], lamz.at[g], s_lz.at[k], r_lz.at[g], to).wait_recv()
    lamx[row] = lse([lamz[g] for g in range(G)])
    for k in range(1, R):
        r, to = xpeer(k)
        go(rcopy(lamx.at[row], lamx.at[row], s_lx.at[k], r_lx.at[row], to))
    for k in range(1, R):
        r, to = xpeer(k)
        rcopy(wm, wm_all.at[r], s_wm.at[k], r_wm.at[r], to).wait_recv()
        rcopy(lamx.at[r], lamx.at[r], s_lx.at[k], r_lx.at[r], to).wait_recv()
    lamz_c[...] = lse([lamx[r] for r in range(R)])

    first = [((c * ND + dep) * R + row) * own for c in (col, sib_col)]

    def delta_chunk(r):
        w = wm_all[r, 0:1, :]
        match = wm_all[r, 1:2, :].astype(jnp.int32)
        scale = w * jnp.exp(m_buf[r] - lamz_c[r])
        part = None
        for h, t in ((0, tgt), (1, T2)):
            ids = lax.broadcasted_iota(jnp.int32, (own, C), 0)
            hit = jnp.where(ids == match - first[h], w, 0.0)
            d = (scale * e_buf[r, h * own:(h + 1) * own, :] - hit).astype(BF16)
            dbuf[r, h * own:(h + 1) * own, :] = d
            q = lax.dot_general(d, t[...], (((0,), (0,)), ((), ())), preferred_element_type=F32)
            part = q if part is None else part + q
        return part

    def part_step(k, carry):
        r, to = xpeer(k)
        ps[r] = delta_chunk(r).astype(BF16).reshape(G, n, D)
        for g in range(G):
            rcopy(ps.at[r, g], px.at[row, g], s_p.at[k, g], r_p.at[row, g], to).start()
        return carry

    lax.fori_loop(1, R, part_step, 0)
    own_part[...] = delta_chunk(row).reshape(G, n, D)

    def gt_half(h):
        def add(r, acc):
            return acc + jnp.dot(dbuf[r, h * own:(h + 1) * own, :], S[r].reshape(C, D),
                                 preferred_element_type=F32)
        acc = jnp.dot(dbuf[0, h * own:(h + 1) * own, :], S[0].reshape(C, D), preferred_element_type=F32)
        for r in range(1, R):
            acc = add(r, acc)
        return acc

    gt_send[...] = gt_half(1)
    go(rcopy(gt_send, gt_recv, s_pair.at[2], r_pair.at[2], sib))

    def stage_sum(g):
        acc = own_part[g]
        for k in range(1, R):
            r, to = xpeer(k)
            rcopy(ps.at[r, g], px.at[r, g], s_p.at[k, g], r_p.at[r, g], to).wait_recv()
            acc = acc + px[r, g].astype(F32)
        return acc

    for k in range(1, G):
        g, to = zpeer(k)
        zs[g] = stage_sum(g).astype(BF16)
        go(rcopy(zs.at[g], zr.at[grp], s_zp.at[k], r_zp.at[grp], to))
    mine = stage_sum(grp)

    gt_out[...] = gt_half(0)
    rcopy(gt_send, gt_recv, s_pair.at[2], r_pair.at[2], sib).wait_recv()
    gt_out[...] = score_scale * (gt_out[...] + gt_recv[...])

    for k in range(1, G):
        g, to = zpeer(k)
        rcopy(zs.at[g], zr.at[g], s_zp.at[k], r_zp.at[g], to).wait_recv()
        mine = mine + zr[g].astype(F32)
    gs_out[...] = score_scale * mine

    for c in sends:
        c.wait_send()
    for k in range(1, R):
        r, to = xpeer(k)
        for g in range(G):
            rcopy(ps.at[r, g], px.at[row, g], s_p.at[k, g], r_p.at[row, g], to).wait_send()


def per_device(R, NC, ND, source_desc, target_desc, target_dual, row_weight, matches):
    n, D = source_desc.shape
    own = target_desc.shape[0]
    G = (NC // 2) * ND
    C = G * n
    par = lax.rem(lax.axis_index("col"), 2)
    dual = lax.dynamic_slice_in_dim(target_dual, lax.axis_index("row") * own, own, 0)[None, :]
    wm = jnp.stack([row_weight, matches.astype(F32)]).reshape(2, NC // 2, 2, ND * n)
    wm = lax.dynamic_index_in_dim(wm, par, 2, keepdims=False).reshape(2, C)
    vm = pl.BlockSpec(memory_space=pltpu.VMEM)
    dma = pltpu.SemaphoreType.DMA
    return pl.pallas_call(
        functools.partial(kernel, R, NC, ND),
        out_shape=(jax.ShapeDtypeStruct((n, D), F32), jax.ShapeDtypeStruct((own, D), F32)),
        in_specs=[vm] * 4,
        out_specs=(vm, vm),
        scratch_shapes=[
            pltpu.VMEM((R, G, n, D), BF16),
            pltpu.VMEM((own, D), BF16),
            pltpu.VMEM((1, own), F32),
            pltpu.VMEM((R, 2, C), F32),
            pltpu.VMEM((2 * own, 128), F32),
            pltpu.VMEM((R, 2 * own, C), F32),
            pltpu.VMEM((R, 1, C), F32),
            pltpu.VMEM((G, R, 1, C), F32),
            pltpu.VMEM((R, R, 1, C), F32),
            pltpu.VMEM((R, 1, C), F32),
            pltpu.VMEM((R, 2 * own, C), BF16),
            pltpu.VMEM((R, G, n, D), BF16),
            pltpu.VMEM((R, G, n, D), BF16),
            pltpu.VMEM((G, n, D), BF16),
            pltpu.VMEM((G, n, D), BF16),
            pltpu.VMEM((G, n, D), F32),
            pltpu.VMEM((own, D), F32),
            pltpu.VMEM((own, D), F32),
            dma((3,)), dma((3,)),
            dma((G,)), dma((G,)),
            dma((R, G)), dma((R, G)),
            dma((R,)), dma((R,)),
            dma((G,)), dma((G,)),
            dma((R,)), dma((R,)),
            dma((R, G)), dma((R, G)),
            dma((G,)), dma((G,)),
        ],
        compiler_params=pltpu.CompilerParams(collective_id=0, has_side_effects=True),
    )(source_desc, target_desc, dual, wm)


def solution(mesh):
    R, NC, ND = mesh.shape["row"], mesh.shape["col"], mesh.shape["depth"]
    return jax.shard_map(
        functools.partial(per_device, R, NC, ND),
        mesh=mesh,
        in_specs=(
            P(("row", "col", "depth"), None),
            P(("col", "depth", "row"), None),
            P(("col", "depth")),
            P("row"),
            P("row"),
        ),
        out_specs=(P(("row", "col", "depth"), None), P(("col", "depth", "row"), None)),
        check_vma=False,
    )
```

```python
import functools
import jax
import jax.numpy as jnp
from jax import lax
from jax.experimental import pallas as pl
from jax.experimental.pallas import tpu as pltpu
from jax.sharding import PartitionSpec as P

score_scale = 0.1875
F32 = jnp.float32
BF16 = jnp.bfloat16


def kernel(R, NC, ND, src, tgt, dual_all, weight, match_in, gs_out, gt_out,
           S, T2, dual, dual2, wm, wm_all, wm_g, dcol, e_buf, m_buf, lamz, lamx, lamz_c, dbuf, ps, px, zs, zr,
           partf, gt_send, gt_recv,
           s_pair, r_pair, s_z, r_z, s_x, r_x, s_wm, r_wm, s_lz, r_lz, s_lx, r_lx, s_p, r_p, s_zp, r_zp):
    G = (NC // 2) * ND
    n, D = src.shape
    own = tgt.shape[0]
    C = R * n
    row = lax.axis_index("row")
    col = lax.axis_index("col")
    dep = lax.axis_index("depth")
    par = lax.rem(col, 2)
    grp = (col // 2) * ND + dep
    sib_col = col + 1 - 2 * par

    def dev(r, c, d):
        return {"row": r, "col": c, "depth": d}

    sib = dev(row, sib_col, dep)

    def xpeer(k):
        r = lax.rem(row + k, R)
        return r, dev(r, col, dep)

    def zpeer(k):
        g = grp
        if G & (G - 1):
            g = lax.rem(grp + k, G)
        else:
            bit = 1
            while bit < G:
                if k & bit:
                    g = g + bit - 2 * bit * lax.rem(g // bit, 2)
                bit *= 2
        return g, dev(row, (g // ND) * 2 + par, lax.rem(g, ND))

    def rcopy(a, b, ss, rs, to):
        return pltpu.make_async_remote_copy(src_ref=a, dst_ref=b, send_sem=ss, recv_sem=rs,
                                            device_id=to, device_id_type=pl.DeviceIdType.MESH)

    barrier = pltpu.get_barrier_semaphore()
    peers = [sib] + [xpeer(k)[1] for k in range(1, R)] + [zpeer(k)[1] for k in range(1, G)]
    for p in peers:
        pl.semaphore_signal(barrier, inc=1, device_id=p, device_id_type=pl.DeviceIdType.MESH)

    S[grp, row] = src[...]
    dual[...] = dual_all[:, pl.ds(pl.multiple_of(row * own, own), own)]
    dcol[0:own, :] = jnp.transpose(jnp.broadcast_to(dual[...], (128, own)))
    for i, vec in ((0, weight[...]), (1, match_in[...].astype(F32))):
        span = ND * n
        parts = [jnp.where(par == 0, vec[:, 2 * c * span:(2 * c + 1) * span],
                           vec[:, (2 * c + 1) * span:(2 * c + 2) * span]) for c in range(NC // 2)]
        wm[i:i + 1, :] = parts[0] if len(parts) == 1 else jnp.concatenate(parts, axis=1)
    wm_all[row] = wm[...]
    pl.semaphore_wait(barrier, len(peers))

    sends = []

    def go(c):
        c.start()
        sends.append(c)

    for k in range(1, G):
        g, to = zpeer(k)
        go(rcopy(src, S.at[grp, row], s_z.at[k], r_z.at[grp], to))
    for k in range(1, R):
        r, to = xpeer(k)
        go(rcopy(src, S.at[grp, row], s_x.at[k, 0], r_x.at[row, grp], to))
    go(rcopy(tgt, T2, s_pair.at[0], r_pair.at[0], sib))
    go(rcopy(dual, dual2, s_pair.at[1], r_pair.at[1], sib))

    def forward(k):
        g, to = zpeer(k)
        rcopy(src, S.at[g, row], s_z.at[k], r_z.at[g], to).wait_recv()
        for j in range(1, R):
            r, xto = xpeer(j)
            go(rcopy(S.at[g, row], S.at[g, row], s_x.at[j, k], r_x.at[row, g], xto))

    forward(1)
    for k in range(1, R):
        r, to = xpeer(k)
        go(rcopy(wm, wm_all.at[row], s_wm.at[k], r_wm.at[row], to))
    rcopy(dual, dual2, s_pair.at[1], r_pair.at[1], sib).wait_recv()
    dcol[own:2 * own, :] = jnp.transpose(jnp.broadcast_to(dual2[...], (128, own)))
    rcopy(tgt, T2, s_pair.at[0], r_pair.at[0], sib).wait_recv()

    lane_rep = C // 128

    def scores_chunk(g):
        rows = S[g].reshape(C, D)
        tops = []
        for h, t in ((0, tgt), (1, T2)):
            p = lax.dot_general(t[...], rows, (((1,), (1,)), ((), ())), preferred_element_type=F32)
            dc = dcol[h * own:(h + 1) * own, :]
            s = score_scale * p + jnp.concatenate([dc] * lane_rep, axis=1)
            e_buf[g, h * own:(h + 1) * own, :] = s
            tops.append(jnp.max(s, axis=0, keepdims=True))
        top = jnp.maximum(tops[0], tops[1])
        m_buf[g] = top
        e = jnp.exp(e_buf[g] - top)
        e_buf[g] = e
        lamz[grp, g] = top + jnp.log(jnp.sum(e, axis=0, keepdims=True))

    for k in range(G):
        g = zpeer(k)[0]
        if 2 <= k + 1 < G:
            forward(k + 1)
        for j in range(1, R):
            r, to = xpeer(j)
            rcopy(src, S.at[g, r], s_x.at[0, 0], r_x.at[r, g], to).wait_recv()
        scores_chunk(g)

    def lse(parts):
        top = functools.reduce(jnp.maximum, parts)
        return top + jnp.log(functools.reduce(jnp.add, [jnp.exp(p - top) for p in parts]))

    for k in range(1, G):
        g, to = zpeer(k)
        go(rcopy(lamz.at[grp], lamz.at[grp], s_lz.at[k], r_lz.at[grp], to))
    for k in range(1, G):
        g, to = zpeer(k)
        rcopy(lamz.at[g], lamz.at[g], s_lz.at[k], r_lz.at[g], to).wait_recv()
    lamx[row] = lse([lamz[g] for g in range(G)])
    for k in range(1, R):
        r, to = xpeer(k)
        go(rcopy(lamx.at[row], lamx.at[row], s_lx.at[k], r_lx.at[row], to))
    for k in range(1, R):
        r, to = xpeer(k)
        rcopy(wm, wm_all.at[r], s_wm.at[k], r_wm.at[r], to).wait_recv()
    for g in range(G):
        for i in range(2):
            wm_g[g, i:i + 1, :] = jnp.concatenate(
                [wm_all[r, i:i + 1, g * n:(g + 1) * n] for r in range(R)], axis=1)
    for k in range(1, R):
        r, to = xpeer(k)
        rcopy(lamx.at[r], lamx.at[r], s_lx.at[k], r_lx.at[r], to).wait_recv()
    lamz_c[...] = lse([lamx[r] for r in range(R)])

    first = [((c * ND + dep) * R + row) * own for c in (col, sib_col)]

    def delta_chunk(g):
        w = wm_g[g, 0:1, :]
        match = wm_g[g, 1:2, :].astype(jnp.int32)
        scale = w * jnp.exp(m_buf[g] - lamz_c[g])
        part = None
        for h, t in ((0, tgt), (1, T2)):
            ids = lax.broadcasted_iota(jnp.int32, (own, C), 0)
            hit = jnp.where(ids == match - first[h], w, 0.0)
            d = (scale * e_buf[g, h * own:(h + 1) * own, :] - hit).astype(BF16)
            dbuf[g, h * own:(h + 1) * own, :] = d
            q = lax.dot_general(d, t[...], (((0,), (0,)), ((), ())), preferred_element_type=F32)
            part = q if part is None else part + q
        return part

    for kz in range(G - 1, -1, -1):
        g = zpeer(kz)[0]
        part = delta_chunk(g).reshape(R, n, D)
        partf[g] = part
        ps[g] = part.astype(BF16)
        for k in range(1, R):
            r, to = xpeer(k)
            go(rcopy(ps.at[g, r], px.at[g, row], s_p.at[k, kz], r_p.at[row, g], to))

    def gt_half(h):
        acc = None
        for g in range(G):
            q = jnp.dot(dbuf[g, h * own:(h + 1) * own, :], S[g].reshape(C, D), preferred_element_type=F32)
            acc = q if acc is None else acc + q
        return acc

    gt_send[...] = gt_half(1)
    go(rcopy(gt_send, gt_recv, s_pair.at[2], r_pair.at[2], sib))

    def stage_sum(g):
        acc = partf[g, row]
        for k in range(1, R):
            r, to = xpeer(k)
            rcopy(ps.at[g, r], px.at[g, r], s_p.at[k, 0], r_p.at[r, g], to).wait_recv()
            acc = acc + px[g, r].astype(F32)
        return acc

    for k in range(G - 1, 0, -1):
        g, to = zpeer(k)
        zs[g] = stage_sum(g).astype(BF16)
        go(rcopy(zs.at[g], zr.at[grp], s_zp.at[k], r_zp.at[grp], to))
    mine = stage_sum(grp)

    gt_out[...] = gt_half(0)
    rcopy(gt_send, gt_recv, s_pair.at[2], r_pair.at[2], sib).wait_recv()
    gt_out[...] = score_scale * (gt_out[...] + gt_recv[...])

    for k in range(1, G):
        g, to = zpeer(k)
        rcopy(zs.at[g], zr.at[g], s_zp.at[k], r_zp.at[g], to).wait_recv()
        mine = mine + zr[g].astype(F32)
    gs_out[...] = score_scale * mine

    for c in sends:
        c.wait_send()


def per_device(R, NC, ND, source_desc, target_desc, target_dual, row_weight, matches):
    n, D = source_desc.shape
    own = target_desc.shape[0]
    G = (NC // 2) * ND
    C = R * n
    vm = pl.BlockSpec(memory_space=pltpu.VMEM)
    dma = pltpu.SemaphoreType.DMA
    return pl.pallas_call(
        functools.partial(kernel, R, NC, ND),
        out_shape=(jax.ShapeDtypeStruct((n, D), F32), jax.ShapeDtypeStruct((own, D), F32)),
        in_specs=[vm] * 5,
        out_specs=(vm, vm),
        scratch_shapes=[
            pltpu.VMEM((G, R, n, D), BF16),
            pltpu.VMEM((own, D), BF16),
            pltpu.VMEM((1, own), F32),
            pltpu.VMEM((1, own), F32),
            pltpu.VMEM((2, G * n), F32),
            pltpu.VMEM((R, 2, G * n), F32),
            pltpu.VMEM((G, 2, C), F32),
            pltpu.VMEM((2 * own, 128), F32),
            pltpu.VMEM((G, 2 * own, C), F32),
            pltpu.VMEM((G, 1, C), F32),
            pltpu.VMEM((G, G, 1, C), F32),
            pltpu.VMEM((R, G, 1, C), F32),
            pltpu.VMEM((G, 1, C), F32),
            pltpu.VMEM((G, 2 * own, C), BF16),
            pltpu.VMEM((G, R, n, D), BF16),
            pltpu.VMEM((G, R, n, D), BF16),
            pltpu.VMEM((G, n, D), BF16),
            pltpu.VMEM((G, n, D), BF16),
            pltpu.VMEM((G, R, n, D), F32),
            pltpu.VMEM((own, D), F32),
            pltpu.VMEM((own, D), F32),
            dma((3,)), dma((3,)),
            dma((G,)), dma((G,)),
            dma((R, G)), dma((R, G)),
            dma((R,)), dma((R,)),
            dma((G,)), dma((G,)),
            dma((R,)), dma((R,)),
            dma((R, G)), dma((R, G)),
            dma((G,)), dma((G,)),
        ],
        compiler_params=pltpu.CompilerParams(collective_id=0, has_side_effects=True,
                                             vmem_limit_bytes=32 * 1024 * 1024),
    )(source_desc, target_desc, target_dual[None, :], row_weight[None, :], matches[None, :])


def solution(mesh):
    R, NC, ND = mesh.shape["row"], mesh.shape["col"], mesh.shape["depth"]
    return jax.shard_map(
        functools.partial(per_device, R, NC, ND),
        mesh=mesh,
        in_specs=(
            P(("row", "col", "depth"), None),
            P(("col", "depth", "row"), None),
            P(("col", "depth")),
            P("row"),
            P("row"),
        ),
        out_specs=(P(("row", "col", "depth"), None), P(("col", "depth", "row"), None)),
        check_vma=False,
    )
```

```python
import functools
import jax
import jax.numpy as jnp
from jax import lax
from jax.experimental import pallas as pl
from jax.experimental.pallas import tpu as pltpu
from jax.sharding import PartitionSpec as P

score_scale = 0.1875
F32 = jnp.float32
BF16 = jnp.bfloat16


def kernel(R, NC, ND, src_h, tgt_h, dual_h, weight_h, match_h, gs_out, gt_out,
           tgt, dual_all, weight, match_in, S, T2, dual, dual2, wm, wm_all, wm_g, dcol, e_buf, m_buf, lam,
           dbuf, ps, px, zs, zr, partf, gt_send, gt_recv,
           s_in, s_pair, r_pair, s_z, r_z, s_x, r_x, s_wm, r_wm, s_l, r_l, s_p, r_p, s_zp, r_zp):
    G = (NC // 2) * ND
    N = R * G
    n, D = src_h.shape
    own = tgt_h.shape[0]
    C = R * n
    row = lax.axis_index("row")
    col = lax.axis_index("col")
    dep = lax.axis_index("depth")
    par = lax.rem(col, 2)
    grp = (col // 2) * ND + dep
    me = grp * R + row
    sib_col = col + 1 - 2 * par
    order = sorted(range(G), key=lambda g: abs(2 * g - G + 1))
    MESH = pl.DeviceIdType.MESH

    def dev(r, c, d):
        return {"row": r, "col": c, "depth": d}

    sib = dev(row, sib_col, dep)

    def xpeer(k):
        r = lax.rem(row + k, R)
        return r, dev(r, col, dep)

    def zdev(g):
        return dev(row, (g // ND) * 2 + par, g % ND)

    def peer(k):
        i = lax.rem(me + k, N)
        g = i // R
        return dev(lax.rem(i, R), (g // ND) * 2 + par, lax.rem(g, ND))

    def rcopy(a, b, ss, rs, to):
        return pltpu.make_async_remote_copy(src_ref=a, dst_ref=b, send_sem=ss, recv_sem=rs,
                                            device_id=to, device_id_type=MESH)

    def each_peer(fn):
        if N <= 32:
            for k in range(1, N):
                fn(k)
        else:
            lax.fori_loop(1, N, lambda k, c: (fn(k), c)[1], 0)

    barrier = pltpu.get_barrier_semaphore()
    pl.semaphore_signal(barrier, inc=1, device_id=sib, device_id_type=MESH)
    each_peer(lambda k: pl.semaphore_signal(barrier, inc=1, device_id=peer(k), device_id_type=MESH))
    loads = [pltpu.make_async_copy(a, b, s_in.at[i]) for i, (a, b) in enumerate((
        (src_h, S.at[grp, row]), (tgt_h, tgt), (dual_h, dual_all), (weight_h, weight), (match_h, match_in)))]
    for c in loads:
        c.start()
    for c in loads:
        c.wait()

    dual[...] = dual_all[:, pl.ds(pl.multiple_of(row * own, own), own)]
    for i, vec in ((0, weight[...]), (1, match_in[...].astype(F32))):
        span = ND * n
        parts = [jnp.where(par == 0, vec[:, 2 * c * span:(2 * c + 1) * span],
                           vec[:, (2 * c + 1) * span:(2 * c + 2) * span]) for c in range(NC // 2)]
        wm[i:i + 1, :] = parts[0] if len(parts) == 1 else jnp.concatenate(parts, axis=1)
    wm_all[row] = wm[...]
    dcol[0:own, :] = jnp.transpose(jnp.broadcast_to(dual[...], (128, own)))
    pl.semaphore_wait(barrier, N)

    sends = []

    def go(c):
        c.start()
        sends.append(c)

    mine_s = S.at[grp, row]

    def z_send(g):
        return rcopy(mine_s, S.at[grp, row], s_z.at[g], r_z.at[grp], zdev(g))

    def x_send(g, j):
        return rcopy(S.at[g, row], S.at[g, row], s_x.at[j, g], r_x.at[row, g], xpeer(j)[1])

    for g in order:
        @pl.when(grp != g)
        def _(g=g):
            z_send(g).start()
    for j in range(1, R):
        x_send(grp, j).start()
    go(rcopy(tgt, T2, s_pair.at[0], r_pair.at[0], sib))
    go(rcopy(dual, dual2, s_pair.at[1], r_pair.at[1], sib))
    for g in order:
        @pl.when(grp != g)
        def _(g=g):
            rcopy(mine_s, S.at[g, row], s_z.at[g], r_z.at[g], zdev(g)).wait_recv()
            for j in range(1, R):
                x_send(g, j).start()
    for k in range(1, R):
        go(rcopy(wm, wm_all.at[row], s_wm.at[k], r_wm.at[row], xpeer(k)[1]))
    rcopy(dual, dual2, s_pair.at[1], r_pair.at[1], sib).wait_recv()
    dcol[own:2 * own, :] = jnp.transpose(jnp.broadcast_to(dual2[...], (128, own)))
    rcopy(tgt, T2, s_pair.at[0], r_pair.at[0], sib).wait_recv()

    lane_rep = C // 128

    def scores_chunk(g):
        rows = S[g].reshape(C, D)
        tops = []
        for h, t in ((0, tgt), (1, T2)):
            p = lax.dot_general(t[...], rows, (((1,), (1,)), ((), ())), preferred_element_type=F32)
            dc = dcol[h * own:(h + 1) * own, :]
            s = score_scale * p + jnp.concatenate([dc] * lane_rep, axis=1)
            e_buf[g, h * own:(h + 1) * own, :] = s
            tops.append(jnp.max(s, axis=0, keepdims=True))
        top = jnp.maximum(tops[0], tops[1])
        m_buf[g] = top
        e = jnp.exp(e_buf[g] - top)
        e_buf[g] = e
        lam[g, me] = top + jnp.log(jnp.sum(e, axis=0, keepdims=True))

    def gather_wait(g):
        for j in range(1, R):
            r, to = xpeer(j)
            rcopy(mine_s, S.at[g, r], s_x.at[0, 0], r_x.at[r, g], to).wait_recv()

    for g in order:
        gather_wait(g)
        scores_chunk(g)
        each_peer(lambda k: rcopy(lam.at[g, me], lam.at[g, me], s_l.at[g], r_l.at[g], peer(k)).start())

    for k in range(1, R):
        r, to = xpeer(k)
        rcopy(wm, wm_all.at[r], s_wm.at[k], r_wm.at[r], to).wait_recv()
    for g in range(G):
        for i in range(2):
            wm_g[g, i:i + 1, :] = jnp.concatenate(
                [wm_all[r, i:i + 1, g * n:(g + 1) * n] for r in range(R)], axis=1)

    first = [((c * ND + dep) * R + row) * own for c in (col, sib_col)]

    def lam_all(g):
        every = lam.at[g, pl.ds(0, N - 1)]
        return rcopy(every, every, s_l.at[g], r_l.at[g], sib)

    def delta_chunk(g):
        lam_all(g).wait_recv()
        parts = lam[g]
        peak = jnp.max(parts, axis=0)
        log_total = peak + jnp.log(jnp.sum(jnp.exp(parts - peak[None]), axis=0))
        w = wm_g[g, 0:1, :]
        match = wm_g[g, 1:2, :].astype(jnp.int32)
        scale = w * jnp.exp(m_buf[g] - log_total)
        part = None
        for h, t in ((0, tgt), (1, T2)):
            ids = lax.broadcasted_iota(jnp.int32, (own, C), 0)
            hit = jnp.where(ids == match - first[h], w, 0.0)
            d = (scale * e_buf[g, h * own:(h + 1) * own, :] - hit).astype(BF16)
            dbuf[g, h * own:(h + 1) * own, :] = d
            q = lax.dot_general(d, t[...], (((0,), (0,)), ((), ())), preferred_element_type=F32)
            part = q if part is None else part + q
        return part

    for g in order:
        part = delta_chunk(g).reshape(R, n, D)
        partf[g] = part
        ps[g] = part.astype(BF16)
        for k in range(1, R):
            r, to = xpeer(k)
            go(rcopy(ps.at[g, r], px.at[g, row], s_p.at[k, g], r_p.at[row, g], to))

    def gt_half(h):
        acc = None
        for g in range(G):
            q = jnp.dot(dbuf[g, h * own:(h + 1) * own, :], S[g].reshape(C, D), preferred_element_type=F32)
            acc = q if acc is None else acc + q
        return acc

    gt_send[...] = gt_half(1)
    go(rcopy(gt_send, gt_recv, s_pair.at[2], r_pair.at[2], sib))

    def stage_sum(g):
        acc = partf[g, row]
        for k in range(1, R):
            acc = acc + px[g, lax.rem(row + k, R)].astype(F32)
        return acc

    def zp_send(g):
        return rcopy(zs.at[g], zr.at[grp], s_zp.at[g], r_zp.at[grp], zdev(g))

    for g in order:
        for k in range(1, R):
            r, to = xpeer(k)
            rcopy(ps.at[g, r], px.at[g, r], s_p.at[k, 0], r_p.at[r, g], to).wait_recv()
        zs[g] = stage_sum(g).astype(BF16)

        @pl.when(grp != g)
        def _(g=g):
            zp_send(g).start()

    gt_out[...] = gt_half(0)
    rcopy(gt_send, gt_recv, s_pair.at[2], r_pair.at[2], sib).wait_recv()
    gt_out[...] = score_scale * (gt_out[...] + gt_recv[...])

    gs_out[...] = stage_sum(grp)
    for g in order:
        @pl.when(grp != g)
        def _(g=g):
            rcopy(zs.at[g], zr.at[g], s_zp.at[g], r_zp.at[g], zdev(g)).wait_recv()
            gs_out[...] = gs_out[...] + zr[g].astype(F32)
    gs_out[...] = score_scale * gs_out[...]

    for c in sends:
        c.wait_send()
    for g in range(G):
        lam_all(g).wait_send()
        for j in range(1, R):
            x_send(g, j).wait_send()

        @pl.when(grp != g)
        def _(g=g):
            z_send(g).wait_send()
            zp_send(g).wait_send()


def per_device(R, NC, ND, source_desc, target_desc, target_dual, row_weight, matches):
    n, D = source_desc.shape
    own = target_desc.shape[0]
    G = (NC // 2) * ND
    C = R * n
    vm = pl.BlockSpec(memory_space=pltpu.VMEM)
    dma = pltpu.SemaphoreType.DMA
    return pl.pallas_call(
        functools.partial(kernel, R, NC, ND),
        out_shape=(jax.ShapeDtypeStruct((n, D), F32), jax.ShapeDtypeStruct((own, D), F32)),
        in_specs=[pl.BlockSpec(memory_space=pltpu.HBM)] * 5,
        out_specs=(vm, vm),
        scratch_shapes=[
            pltpu.VMEM((own, D), BF16),
            pltpu.VMEM((1, target_dual.shape[0]), F32),
            pltpu.VMEM((1, row_weight.shape[0]), F32),
            pltpu.VMEM((1, row_weight.shape[0]), jnp.int32),
            pltpu.VMEM((G, R, n, D), BF16),
            pltpu.VMEM((own, D), BF16),
            pltpu.VMEM((1, own), F32),
            pltpu.VMEM((1, own), F32),
            pltpu.VMEM((2, G * n), F32),
            pltpu.VMEM((R, 2, G * n), F32),
            pltpu.VMEM((G, 2, C), F32),
            pltpu.VMEM((2 * own, 128), F32),
            pltpu.VMEM((G, 2 * own, C), F32),
            pltpu.VMEM((G, 1, C), F32),
            pltpu.VMEM((G, R * G, 1, C), F32),
            pltpu.VMEM((G, 2 * own, C), BF16),
            pltpu.VMEM((G, R, n, D), BF16),
            pltpu.VMEM((G, R, n, D), BF16),
            pltpu.VMEM((G, n, D), BF16),
            pltpu.VMEM((G, n, D), BF16),
            pltpu.VMEM((G, R, n, D), F32),
            pltpu.VMEM((own, D), F32),
            pltpu.VMEM((own, D), F32),
            dma((5,)),
            dma((3,)), dma((3,)),
            dma((G,)), dma((G,)),
            dma((R, G)), dma((R, G)),
            dma((R,)), dma((R,)),
            dma((G,)), dma((G,)),
            dma((R, G)), dma((R, G)),
            dma((G,)), dma((G,)),
        ],
        compiler_params=pltpu.CompilerParams(collective_id=0, has_side_effects=True,
                                             vmem_limit_bytes=32 * 1024 * 1024),
    )(source_desc, target_desc, target_dual[None, :], row_weight[None, :], matches[None, :])


def solution(mesh):
    R, NC, ND = mesh.shape["row"], mesh.shape["col"], mesh.shape["depth"]
    return jax.shard_map(
        functools.partial(per_device, R, NC, ND),
        mesh=mesh,
        in_specs=(
            P(("row", "col", "depth"), None),
            P(("col", "depth", "row"), None),
            P(("col", "depth")),
            P("row"),
            P("row"),
        ),
        out_specs=(P(("row", "col", "depth"), None), P(("col", "depth", "row"), None)),
        check_vma=False,
    )
```

```python
import functools
import jax
import jax.numpy as jnp
from jax import lax
from jax.experimental import pallas as pl
from jax.experimental.pallas import tpu as pltpu
from jax.sharding import PartitionSpec as P

score_scale = 0.1875
F32 = jnp.float32
BF16 = jnp.bfloat16


def kernel(R, NC, ND, src_h, tgt_h, dual_h, weight_h, match_h, gs_out, gt_out,
           tgt, dual_all, weight, match_in, S, T2, dual, dual2, wm, wm_all, wm_g, dcol, e_buf, m_buf, lam,
           dbuf, ps, px, zs, zr, partf, gt_send, gt_recv,
           s_in, s_pair, r_pair, s_z, r_z, s_x, r_x, s_wm, r_wm, s_l, r_l, s_p, r_p, s_zp, r_zp, line_in):
    G = (NC // 2) * ND
    N = R * G
    n, D = src_h.shape
    own = tgt_h.shape[0]
    C = R * n
    row = lax.axis_index("row")
    col = lax.axis_index("col")
    dep = lax.axis_index("depth")
    par = lax.rem(col, 2)
    grp = (col // 2) * ND + dep
    me = grp * R + row
    sib_col = col + 1 - 2 * par
    order = sorted(range(G), key=lambda g: abs(2 * g - G + 1))
    MESH = pl.DeviceIdType.MESH

    def dev(r, c, d):
        return {"row": r, "col": c, "depth": d}

    sib = dev(row, sib_col, dep)

    def xpeer(k):
        return ring[k], dev(ring[k], col, dep)

    def zdev(g):
        return dev(row, (g // ND) * 2 + par, g % ND)

    def peer(k):
        i = lax.rem(me + k, N)
        g = i // R
        return dev(lax.rem(i, R), (g // ND) * 2 + par, lax.rem(g, ND))

    def rcopy(a, b, ss, rs, to):
        return pltpu.make_async_remote_copy(src_ref=a, dst_ref=b, send_sem=ss, recv_sem=rs,
                                            device_id=to, device_id_type=MESH)

    ring = [lax.rem(row + j, R) for j in range(R)]

    def each_peer(fn):
        if N <= 32:
            for g in range(G):
                for j in range(R - 1, 0, -1):
                    fn(dev(ring[j], (g // ND) * 2 + par, g % ND))

                @pl.when(grp != g)
                def _(g=g):
                    fn(zdev(g))
        else:
            lax.fori_loop(1, N, lambda k, c: (fn(peer(k)), c)[1], 0)

    barrier = pltpu.get_barrier_semaphore()
    pl.semaphore_signal(barrier, inc=1, device_id=sib, device_id_type=MESH)
    for j in range(1, R):
        pl.semaphore_signal(barrier, inc=1, device_id=xpeer(j)[1], device_id_type=MESH)
    for g in range(G):
        @pl.when(grp != g)
        def _(g=g):
            pl.semaphore_signal(barrier, inc=1, device_id=zdev(g), device_id_type=MESH)
    loads = [pltpu.make_async_copy(a, b, s_in.at[i]) for i, (a, b) in enumerate((
        (src_h, S.at[grp, row]), (tgt_h, tgt), (dual_h, dual_all), (weight_h, weight), (match_h, match_in)))]
    for c in loads:
        c.start()
    for c in loads[2:]:
        c.wait()

    dual[...] = dual_all[:, pl.ds(pl.multiple_of(row * own, own), own)]
    for i, vec in ((0, weight[...]), (1, match_in[...].astype(F32))):
        span = ND * n
        parts = [jnp.where(par == 0, vec[:, 2 * c * span:(2 * c + 1) * span],
                           vec[:, (2 * c + 1) * span:(2 * c + 2) * span]) for c in range(NC // 2)]
        wm[i:i + 1, :] = parts[0] if len(parts) == 1 else jnp.concatenate(parts, axis=1)
    wm_all[row] = wm[...]
    dcol[0:own, :] = jnp.transpose(jnp.broadcast_to(dual[...], (128, own)))
    for c in loads[:2]:
        c.wait()
    pl.semaphore_wait(barrier, R + G - 1)

    sends = []

    def go(c):
        c.start()
        sends.append(c)

    mine_s = S.at[grp, row]

    def z_send(g):
        return rcopy(mine_s, S.at[grp, row], s_z.at[g], r_z.at[grp], zdev(g))

    def x_send(g, j):
        return rcopy(S.at[g, row], S.at[g, row], s_x.at[j, g], r_x.at[row, g], xpeer(j)[1])

    for g in order:
        @pl.when(grp != g)
        def _(g=g):
            z_send(g).start()
    for j in range(1, R):
        x_send(grp, j).start()
    go(rcopy(tgt, T2, s_pair.at[0], r_pair.at[0], sib))
    go(rcopy(dual, dual2, s_pair.at[1], r_pair.at[1], sib))
    for g in order:
        @pl.when(grp != g)
        def _(g=g):
            rcopy(mine_s, S.at[g, row], s_z.at[g], r_z.at[g], zdev(g)).wait_recv()
            for j in range(1, R):
                x_send(g, j).start()
    for k in range(1, R):
        pl.semaphore_signal(line_in, inc=1, device_id=xpeer(k)[1], device_id_type=MESH)
        go(rcopy(wm, wm_all.at[row], s_wm.at[k], r_wm.at[row], xpeer(k)[1]))
    rcopy(dual, dual2, s_pair.at[1], r_pair.at[1], sib).wait_recv()
    dcol[own:2 * own, :] = jnp.transpose(jnp.broadcast_to(dual2[...], (128, own)))
    rcopy(tgt, T2, s_pair.at[0], r_pair.at[0], sib).wait_recv()

    lane_rep = C // 128

    def scores_chunk(g):
        rows = S[g].reshape(C, D)
        tops = []
        for h, t in ((0, tgt), (1, T2)):
            p = lax.dot_general(t[...], rows, (((1,), (1,)), ((), ())), preferred_element_type=F32)
            dc = dcol[h * own:(h + 1) * own, :]
            s = score_scale * p + jnp.concatenate([dc] * lane_rep, axis=1)
            e_buf[g, h * own:(h + 1) * own, :] = s
            tops.append(jnp.max(s, axis=0, keepdims=True))
        top = jnp.maximum(tops[0], tops[1])
        m_buf[g] = top
        e = jnp.exp(e_buf[g] - top)
        e_buf[g] = e
        lam[g, me] = top + jnp.log(jnp.sum(e, axis=0, keepdims=True))

    def gather_wait(g):
        for j in range(1, R):
            r, to = xpeer(j)
            rcopy(mine_s, S.at[g, r], s_x.at[0, 0], r_x.at[r, g], to).wait_recv()

    for i, g in enumerate(order):
        gather_wait(g)
        scores_chunk(g)
        if i == 0:
            pl.semaphore_wait(line_in, R - 1)
        each_peer(lambda to: rcopy(lam.at[g, me], lam.at[g, me], s_l.at[g], r_l.at[g], to).start())

    for k in range(1, R):
        r, to = xpeer(k)
        rcopy(wm, wm_all.at[r], s_wm.at[k], r_wm.at[r], to).wait_recv()
    for g in range(G):
        for i in range(2):
            wm_g[g, i:i + 1, :] = jnp.concatenate(
                [wm_all[r, i:i + 1, g * n:(g + 1) * n] for r in range(R)], axis=1)

    first = [((c * ND + dep) * R + row) * own for c in (col, sib_col)]

    def lam_all(g):
        every = lam.at[g, pl.ds(0, N - 1)]
        return rcopy(every, every, s_l.at[g], r_l.at[g], sib)

    def delta_chunk(g):
        lam_all(g).wait_recv()
        parts = lam[g]
        peak = jnp.max(parts, axis=0)
        log_total = peak + jnp.log(jnp.sum(jnp.exp(parts - peak[None]), axis=0))
        w = wm_g[g, 0:1, :]
        match = wm_g[g, 1:2, :].astype(jnp.int32)
        scale = w * jnp.exp(m_buf[g] - log_total)
        part = None
        for h, t in ((0, tgt), (1, T2)):
            ids = lax.broadcasted_iota(jnp.int32, (own, C), 0)
            hit = jnp.where(ids == match - first[h], w, 0.0)
            d = (scale * e_buf[g, h * own:(h + 1) * own, :] - hit).astype(BF16)
            dbuf[g, h * own:(h + 1) * own, :] = d
            q = lax.dot_general(d, t[...], (((0,), (0,)), ((), ())), preferred_element_type=F32)
            part = q if part is None else part + q
        return part

    for g in order:
        part = delta_chunk(g).reshape(R, n, D)
        partf[g] = part
        ps[g] = part.astype(BF16)
        for k in range(1, R):
            r, to = xpeer(k)
            go(rcopy(ps.at[g, r], px.at[g, row], s_p.at[k, g], r_p.at[row, g], to))

    def gt_half(h):
        acc = None
        for g in range(G):
            q = jnp.dot(dbuf[g, h * own:(h + 1) * own, :], S[g].reshape(C, D), preferred_element_type=F32)
            acc = q if acc is None else acc + q
        return acc

    gt_send[...] = gt_half(1)
    go(rcopy(gt_send, gt_recv, s_pair.at[2], r_pair.at[2], sib))

    def stage_sum(g):
        acc = partf[g, row]
        for k in range(1, R):
            acc = acc + px[g, ring[k]].astype(F32)
        return acc

    def zp_send(g):
        return rcopy(zs.at[g], zr.at[grp], s_zp.at[g], r_zp.at[grp], zdev(g))

    for g in order:
        for k in range(1, R):
            r, to = xpeer(k)
            rcopy(ps.at[g, r], px.at[g, r], s_p.at[k, 0], r_p.at[r, g], to).wait_recv()
        zs[g] = stage_sum(g).astype(BF16)

        @pl.when(grp != g)
        def _(g=g):
            zp_send(g).start()

    gt_out[...] = gt_half(0)
    rcopy(gt_send, gt_recv, s_pair.at[2], r_pair.at[2], sib).wait_recv()
    gt_out[...] = score_scale * (gt_out[...] + gt_recv[...])

    gs_out[...] = stage_sum(grp)
    for g in order:
        @pl.when(grp != g)
        def _(g=g):
            rcopy(zs.at[g], zr.at[g], s_zp.at[g], r_zp.at[g], zdev(g)).wait_recv()
            gs_out[...] = gs_out[...] + zr[g].astype(F32)
    gs_out[...] = score_scale * gs_out[...]

    for c in sends:
        c.wait_send()
    for g in range(G):
        lam_all(g).wait_send()
        for j in range(1, R):
            x_send(g, j).wait_send()

        @pl.when(grp != g)
        def _(g=g):
            z_send(g).wait_send()
            zp_send(g).wait_send()


def per_device(R, NC, ND, source_desc, target_desc, target_dual, row_weight, matches):
    n, D = source_desc.shape
    own = target_desc.shape[0]
    G = (NC // 2) * ND
    C = R * n
    vm = pl.BlockSpec(memory_space=pltpu.VMEM)
    dma = pltpu.SemaphoreType.DMA
    return pl.pallas_call(
        functools.partial(kernel, R, NC, ND),
        out_shape=(jax.ShapeDtypeStruct((n, D), F32), jax.ShapeDtypeStruct((own, D), F32)),
        in_specs=[pl.BlockSpec(memory_space=pltpu.HBM)] * 5,
        out_specs=(vm, vm),
        scratch_shapes=[
            pltpu.VMEM((own, D), BF16),
            pltpu.VMEM((1, target_dual.shape[0]), F32),
            pltpu.VMEM((1, row_weight.shape[0]), F32),
            pltpu.VMEM((1, row_weight.shape[0]), jnp.int32),
            pltpu.VMEM((G, R, n, D), BF16),
            pltpu.VMEM((own, D), BF16),
            pltpu.VMEM((1, own), F32),
            pltpu.VMEM((1, own), F32),
            pltpu.VMEM((2, G * n), F32),
            pltpu.VMEM((R, 2, G * n), F32),
            pltpu.VMEM((G, 2, C), F32),
            pltpu.VMEM((2 * own, 128), F32),
            pltpu.VMEM((G, 2 * own, C), F32),
            pltpu.VMEM((G, 1, C), F32),
            pltpu.VMEM((G, R * G, 1, C), F32),
            pltpu.VMEM((G, 2 * own, C), BF16),
            pltpu.VMEM((G, R, n, D), BF16),
            pltpu.VMEM((G, R, n, D), BF16),
            pltpu.VMEM((G, n, D), BF16),
            pltpu.VMEM((G, n, D), BF16),
            pltpu.VMEM((G, R, n, D), F32),
            pltpu.VMEM((own, D), F32),
            pltpu.VMEM((own, D), F32),
            dma((5,)),
            dma((3,)), dma((3,)),
            dma((G,)), dma((G,)),
            dma((R, G)), dma((R, G)),
            dma((R,)), dma((R,)),
            dma((G,)), dma((G,)),
            dma((R, G)), dma((R, G)),
            dma((G,)), dma((G,)),
            pltpu.SemaphoreType.REGULAR,
        ],
        compiler_params=pltpu.CompilerParams(collective_id=0, has_side_effects=True,
                                             vmem_limit_bytes=32 * 1024 * 1024),
    )(*[pltpu.with_memory_space_constraint(a, pltpu.HBM) for a in (
        source_desc, target_desc, target_dual[None, :], row_weight[None, :], matches[None, :])])


def solution(mesh):
    R, NC, ND = mesh.shape["row"], mesh.shape["col"], mesh.shape["depth"]
    return jax.shard_map(
        functools.partial(per_device, R, NC, ND),
        mesh=mesh,
        in_specs=(
            P(("row", "col", "depth"), None),
            P(("col", "depth", "row"), None),
            P(("col", "depth")),
            P("row"),
            P("row"),
        ),
        out_specs=(P(("row", "col", "depth"), None), P(("col", "depth", "row"), None)),
        check_vma=False,
    )
```

```python
import functools
import jax
import jax.numpy as jnp
from jax import lax
from jax.experimental import pallas as pl
from jax.experimental.pallas import tpu as pltpu
from jax.sharding import PartitionSpec as P

score_scale = 0.1875
F32 = jnp.float32
BF16 = jnp.bfloat16


def kernel(R, NC, ND, src_h, tgt_h, dual_h, weight_h, match_h, gs_out, gt_out,
           tgt, dual_all, weight, match_in, S, T2, dual, dual2, wm, wm_all, wm_g, dcol, e_buf, m_buf, lam,
           dbuf, ps, px, zs, zr, partf, gt_send, gt_recv,
           s_in, s_pair, r_pair, s_z, r_z, s_x, r_x, s_wm, r_wm, s_l, r_l, s_p, r_p, s_zp, r_zp, line_in):
    G = (NC // 2) * ND
    N = R * G
    n, D = src_h.shape
    own = tgt_h.shape[0]
    C = R * n
    row = lax.axis_index("row")
    col = lax.axis_index("col")
    dep = lax.axis_index("depth")
    par = lax.rem(col, 2)
    grp = (col // 2) * ND + dep
    me = grp * R + row
    sib_col = col + 1 - 2 * par
    order = sorted(range(G), key=lambda g: abs(2 * g - G + 1))
    MESH = pl.DeviceIdType.MESH

    def dev(r, c, d):
        return {"row": r, "col": c, "depth": d}

    sib = dev(row, sib_col, dep)

    def xpeer(k):
        return ring[k], dev(ring[k], col, dep)

    def zdev(g):
        return dev(row, (g // ND) * 2 + par, g % ND)

    def peer(k):
        i = lax.rem(me + k, N)
        g = i // R
        return dev(lax.rem(i, R), (g // ND) * 2 + par, lax.rem(g, ND))

    def rcopy(a, b, ss, rs, to):
        return pltpu.make_async_remote_copy(src_ref=a, dst_ref=b, send_sem=ss, recv_sem=rs,
                                            device_id=to, device_id_type=MESH)

    ring = [lax.rem(row + j, R) for j in range(R)]

    def each_peer(fn):
        if N <= 32:
            for g in range(G):
                for j in range(R - 1, 0, -1):
                    fn(dev(ring[j], (g // ND) * 2 + par, g % ND))

                @pl.when(grp != g)
                def _(g=g):
                    fn(zdev(g))
        else:
            lax.fori_loop(1, N, lambda k, c: (fn(peer(k)), c)[1], 0)

    barrier = pltpu.get_barrier_semaphore()
    pl.semaphore_signal(barrier, inc=1, device_id=sib, device_id_type=MESH)
    for j in range(1, R):
        pl.semaphore_signal(barrier, inc=1, device_id=xpeer(j)[1], device_id_type=MESH)
    for g in range(G):
        @pl.when(grp != g)
        def _(g=g):
            pl.semaphore_signal(barrier, inc=1, device_id=zdev(g), device_id_type=MESH)
    loads = [pltpu.make_async_copy(a, b, s_in.at[i]) for i, (a, b) in enumerate((
        (src_h, S.at[grp, row]), (tgt_h, tgt), (dual_h, dual_all), (weight_h, weight), (match_h, match_in)))]
    for c in loads:
        c.start()
    for c in loads[2:]:
        c.wait()

    dual[...] = dual_all[:, pl.ds(pl.multiple_of(row * own, own), own)]
    for i, vec in ((0, weight[...]), (1, match_in[...].astype(F32))):
        span = ND * n
        parts = [jnp.where(par == 0, vec[:, 2 * c * span:(2 * c + 1) * span],
                           vec[:, (2 * c + 1) * span:(2 * c + 2) * span]) for c in range(NC // 2)]
        wm[i:i + 1, :] = parts[0] if len(parts) == 1 else jnp.concatenate(parts, axis=1)
    wm_all[row] = wm[...]
    dcol[0:own, :] = jnp.transpose(jnp.broadcast_to(dual[...], (128, own)))
    for c in loads[:2]:
        c.wait()
    pl.semaphore_wait(barrier, R + G - 1)

    sends = []

    def go(c):
        c.start()
        sends.append(c)

    mine_s = S.at[grp, row]

    def z_send(g):
        return rcopy(mine_s, S.at[grp, row], s_z.at[g], r_z.at[grp], zdev(g))

    def x_send(g, j):
        return rcopy(S.at[g, row], S.at[g, row], s_x.at[j, g], r_x.at[row, g], xpeer(j)[1])

    for g in order:
        @pl.when(grp != g)
        def _(g=g):
            z_send(g).start()
    for j in range(1, R):
        x_send(grp, j).start()
    go(rcopy(tgt, T2, s_pair.at[0], r_pair.at[0], sib))
    go(rcopy(dual, dual2, s_pair.at[1], r_pair.at[1], sib))
    for g in order:
        @pl.when(grp != g)
        def _(g=g):
            rcopy(mine_s, S.at[g, row], s_z.at[g], r_z.at[g], zdev(g)).wait_recv()
            for j in range(1, R):
                x_send(g, j).start()
    for k in range(1, R):
        pl.semaphore_signal(line_in, inc=1, device_id=xpeer(k)[1], device_id_type=MESH)
        go(rcopy(wm, wm_all.at[row], s_wm.at[k], r_wm.at[row], xpeer(k)[1]))
    rcopy(dual, dual2, s_pair.at[1], r_pair.at[1], sib).wait_recv()
    dcol[own:2 * own, :] = jnp.transpose(jnp.broadcast_to(dual2[...], (128, own)))
    rcopy(tgt, T2, s_pair.at[0], r_pair.at[0], sib).wait_recv()

    lane_rep = C // 128

    def scores_chunk(g):
        rows = S[g].reshape(C, D)
        tops = []
        for h, t in ((0, tgt), (1, T2)):
            p = lax.dot_general(t[...], rows, (((1,), (1,)), ((), ())), preferred_element_type=F32)
            dc = dcol[h * own:(h + 1) * own, :]
            s = score_scale * p + jnp.concatenate([dc] * lane_rep, axis=1)
            e_buf[g, h * own:(h + 1) * own, :] = s
            tops.append(jnp.max(s, axis=0, keepdims=True))
        top = jnp.maximum(tops[0], tops[1])
        m_buf[g] = top
        e = jnp.exp(e_buf[g] - top)
        e_buf[g] = e
        lam[g, me] = top + jnp.log(jnp.sum(e, axis=0, keepdims=True))

    def gather_wait(g):
        for j in range(1, R):
            r, to = xpeer(j)
            rcopy(mine_s, S.at[g, r], s_x.at[0, 0], r_x.at[r, g], to).wait_recv()

    for i, g in enumerate(order):
        gather_wait(g)
        scores_chunk(g)
        if i == 0:
            pl.semaphore_wait(line_in, R - 1)
        each_peer(lambda to: rcopy(lam.at[g, me], lam.at[g, me], s_l.at[g], r_l.at[g], to).start())

    for k in range(1, R):
        r, to = xpeer(k)
        rcopy(wm, wm_all.at[r], s_wm.at[k], r_wm.at[r], to).wait_recv()
    for g in range(G):
        for i in range(2):
            wm_g[g, i:i + 1, :] = jnp.concatenate(
                [wm_all[r, i:i + 1, g * n:(g + 1) * n] for r in range(R)], axis=1)

    first = [((c * ND + dep) * R + row) * own for c in (col, sib_col)]

    def lam_all(g):
        every = lam.at[g, pl.ds(0, N - 1)]
        return rcopy(every, every, s_l.at[g], r_l.at[g], sib)

    def delta_chunk(g):
        lam_all(g).wait_recv()
        parts = lam[g]
        peak = jnp.max(parts, axis=0)
        log_total = peak + jnp.log(jnp.sum(jnp.exp(parts - peak[None]), axis=0))
        w = wm_g[g, 0:1, :]
        match = wm_g[g, 1:2, :].astype(jnp.int32)
        scale = w * jnp.exp(m_buf[g] - log_total)
        part = None
        for h, t in ((0, tgt), (1, T2)):
            ids = lax.broadcasted_iota(jnp.int32, (own, C), 0)
            hit = jnp.where(ids == match - first[h], w, 0.0)
            d = (scale * e_buf[g, h * own:(h + 1) * own, :] - hit).astype(BF16)
            dbuf[g, h * own:(h + 1) * own, :] = d
            q = lax.dot_general(d, t[...], (((0,), (0,)), ((), ())), preferred_element_type=F32)
            part = q if part is None else part + q
        return part

    for g in order:
        part = delta_chunk(g).reshape(R, n, D)
        partf[g] = part
        ps[g] = part.astype(BF16)
        for k in range(1, R):
            r, to = xpeer(k)
            go(rcopy(ps.at[g, r], px.at[g, row], s_p.at[k, g], r_p.at[row, g], to))

    def gt_half(h):
        acc = None
        for g in range(G):
            q = jnp.dot(dbuf[g, h * own:(h + 1) * own, :], S[g].reshape(C, D), preferred_element_type=F32)
            acc = q if acc is None else acc + q
        return acc

    gt_send[...] = gt_half(1)
    go(rcopy(gt_send, gt_recv, s_pair.at[2], r_pair.at[2], sib))

    def stage_sum(g):
        acc = partf[g, row]
        for k in range(1, R):
            acc = acc + px[g, ring[k]].astype(F32)
        return acc

    def zp_send(g):
        return rcopy(zs.at[g], zr.at[grp], s_zp.at[g], r_zp.at[grp], zdev(g))

    for g in order:
        for k in range(1, R):
            r, to = xpeer(k)
            rcopy(ps.at[g, r], px.at[g, r], s_p.at[k, 0], r_p.at[r, g], to).wait_recv()
        zs[g] = stage_sum(g).astype(BF16)

        @pl.when(grp != g)
        def _(g=g):
            zp_send(g).start()

    gt_out[...] = gt_half(0)
    rcopy(gt_send, gt_recv, s_pair.at[2], r_pair.at[2], sib).wait_recv()
    gt_out[...] = score_scale * (gt_out[...] + gt_recv[...])

    gs_out[...] = stage_sum(grp)
    for g in order:
        @pl.when(grp != g)
        def _(g=g):
            rcopy(zs.at[g], zr.at[g], s_zp.at[g], r_zp.at[g], zdev(g)).wait_recv()
            gs_out[...] = gs_out[...] + zr[g].astype(F32)
    gs_out[...] = score_scale * gs_out[...]

    for c in sends:
        c.wait_send()
    for g in range(G):
        lam_all(g).wait_send()
        for j in range(1, R):
            x_send(g, j).wait_send()

        @pl.when(grp != g)
        def _(g=g):
            z_send(g).wait_send()
            zp_send(g).wait_send()


def flush(gs, gt, gs_out, gt_out, sem):
    copies = [pltpu.make_async_copy(gt, gt_out, sem.at[0]), pltpu.make_async_copy(gs, gs_out, sem.at[1])]
    for c in copies:
        c.start()
    for c in copies:
        c.wait()


def per_device(R, NC, ND, source_desc, target_desc, target_dual, row_weight, matches):
    n, D = source_desc.shape
    own = target_desc.shape[0]
    G = (NC // 2) * ND
    C = R * n
    vm = pl.BlockSpec(memory_space=pltpu.VMEM)
    dma = pltpu.SemaphoreType.DMA
    outs = pl.pallas_call(
        functools.partial(kernel, R, NC, ND),
        out_shape=(jax.ShapeDtypeStruct((n, D), F32), jax.ShapeDtypeStruct((own, D), F32)),
        in_specs=[pl.BlockSpec(memory_space=pltpu.HBM)] * 5,
        out_specs=(vm, vm),
        scratch_shapes=[
            pltpu.VMEM((own, D), BF16),
            pltpu.VMEM((1, target_dual.shape[0]), F32),
            pltpu.VMEM((1, row_weight.shape[0]), F32),
            pltpu.VMEM((1, row_weight.shape[0]), jnp.int32),
            pltpu.VMEM((G, R, n, D), BF16),
            pltpu.VMEM((own, D), BF16),
            pltpu.VMEM((1, own), F32),
            pltpu.VMEM((1, own), F32),
            pltpu.VMEM((2, G * n), F32),
            pltpu.VMEM((R, 2, G * n), F32),
            pltpu.VMEM((G, 2, C), F32),
            pltpu.VMEM((2 * own, 128), F32),
            pltpu.VMEM((G, 2 * own, C), F32),
            pltpu.VMEM((G, 1, C), F32),
            pltpu.VMEM((G, R * G, 1, C), F32),
            pltpu.VMEM((G, 2 * own, C), BF16),
            pltpu.VMEM((G, R, n, D), BF16),
            pltpu.VMEM((G, R, n, D), BF16),
            pltpu.VMEM((G, n, D), BF16),
            pltpu.VMEM((G, n, D), BF16),
            pltpu.VMEM((G, R, n, D), F32),
            pltpu.VMEM((own, D), F32),
            pltpu.VMEM((own, D), F32),
            dma((5,)),
            dma((3,)), dma((3,)),
            dma((G,)), dma((G,)),
            dma((R, G)), dma((R, G)),
            dma((R,)), dma((R,)),
            dma((G,)), dma((G,)),
            dma((R, G)), dma((R, G)),
            dma((G,)), dma((G,)),
            pltpu.SemaphoreType.REGULAR,
        ],
        compiler_params=pltpu.CompilerParams(collective_id=0, has_side_effects=True,
                                             vmem_limit_bytes=32 * 1024 * 1024),
    )(*[pltpu.with_memory_space_constraint(a, pltpu.HBM) for a in (
        source_desc, target_desc, target_dual[None, :], row_weight[None, :], matches[None, :])])
    hbm = pl.BlockSpec(memory_space=pltpu.HBM)
    return pl.pallas_call(
        flush,
        out_shape=(jax.ShapeDtypeStruct((n, D), F32), jax.ShapeDtypeStruct((own, D), F32)),
        in_specs=[vm, vm],
        out_specs=(hbm, hbm),
        scratch_shapes=[dma((2,))],
        compiler_params=pltpu.CompilerParams(vmem_limit_bytes=8 * 1024 * 1024),
    )(*outs)


def solution(mesh):
    R, NC, ND = mesh.shape["row"], mesh.shape["col"], mesh.shape["depth"]
    return jax.shard_map(
        functools.partial(per_device, R, NC, ND),
        mesh=mesh,
        in_specs=(
            P(("row", "col", "depth"), None),
            P(("col", "depth", "row"), None),
            P(("col", "depth")),
            P("row"),
            P("row"),
        ),
        out_specs=(P(("row", "col", "depth"), None), P(("col", "depth", "row"), None)),
        check_vma=False,
    )
```
